32 devices in a mesh: lat: 4 (over y, x), lev: 8 (over z, core).
Axes of the slice: x: 2, y: 2, z: 4, core: 2. Of those that a mesh axis runs over, the one named last changes fastest.
Arguments:
- tracers: float32 [2, 128, 64, 128], P(None, 'lev', 'lat'), may hold values from -6 to 6
- layer_mass: float32 [128, 64, 128], P('lev', 'lat'), may hold values from 0.5 to 2
- courant: float32 [128, 64], P('lev', 'lat'), may hold values from 0.1 to 0.9
- remap: float32 [128, 128], replicated, may hold values from 0 to 1, as said below
- cost_class: int32 [64, 128], P('lat', 'lev'), may hold values from 0 to 2
- spans: int32 [512, 1], P(('lat', 'lev')), may hold values from 0 to 3; in each aligned block of 16 rows (0 to 15, 16 to 31, ...) at most 4 rows name the same one
- w_up: bfloat16 [4, 256, 512], P('lat'), may hold values from -0.375 to 0.375
- b_up: float32 [4, 512], P('lat'), may hold values from -6 to 6
- w_mid: bfloat16 [4, 512, 512], P('lat'), may hold values from -0.25 to 0.25
- w_down: bfloat16 [4, 512, 256], P('lat'), may hold values from -0.25 to 0.25
- sw_up: bfloat16 [4, 256, 512], P('lat'), may hold values from -0.375 to 0.375
- sw_down: bfloat16 [4, 512, 256], P('lat'), may hold values from -0.25 to 0.25
Outputs:
- tracers_out: float32 [2, 128, 64, 128], P(None, None, 'lat', 'lev')
The draws below stay inside these ranges and needn't reach their ends.
Inputs may be any that keep to these rules, and one draw needn't show every extreme that they name: `remap`: diagonal entries are 1, the others lie between 0 and 1 / 128. `spans`: among the 16 rows of one device (aligned blocks of 16 rows, in the order of the devices along lat then lev), no value appears more than 4 times, and one value appears exactly 4 times.
All inputs are finite; a program needn't handle non-finite values.
Results may differ from the reference program's by a relative error of at most 0.005.
Values may be sent and summed in bfloat16 or wider, within the bound.
A program may use at most 64 MiB of HBM per device.

```python
import math
import jax
import jax.numpy as jnp
import numpy as np
from jax import lax

LEV = 128
HID = 512
SUBSTEPS = 4
BLK = 16
LAT_DEV = 16
LON_DEV = 16
LAT = 64
LON = 128
F = 256
EXPERTS = 4
BLOCKS_DEV = 16
MOST = 4
NBLK = 512
N_LAT = 4
N_LEV = 8


def draw_remap(key, part):
    spread_off = jax.random.uniform(key, (LEV, LEV), jnp.float32, 0.0, 1.0 / LEV)
    unit_diag = jnp.eye(LEV, dtype=jnp.float32)
    return spread_off * (1.0 - unit_diag) + unit_diag


def with_ends(result, stream_key, least, top_value):
    longest = result.shape.index(max(result.shape))
    spots = []
    for shift in (0, 1):
        where = [jax.random.randint(jax.random.fold_in(stream_key, axis), (), 0, length) for axis, length in enumerate(result.shape)]
        where[longest] = (where[longest] + shift) % result.shape[longest]
        spots.append(tuple(where))
    return result.at[spots[0]].set(least).at[spots[1]].set(top_value)


def shard_levels(key, extent, split, smallest, high):
    level = 1.0
    for dim, parts in split:
        draws = jax.random.uniform(jax.random.fold_in(jax.random.fold_in(key, 6), dim), (parts,), jnp.float32, smallest / len(split), high / len(split))
        level = level * jnp.repeat(jnp.exp(draws), extent[dim] // parts).reshape((-1,) + (1,) * (len(extent) - 1 - dim))
    return level


def shared_out(own_key, own, number, rows, count, top, bound, lean):
    sequence = jax.random.permutation(own_key, count)
    packed, ordinary = shares(count, rows * top, bound, lean, True), shares(count, rows * top, bound, lean, False)
    places = jnp.arange(count)

    def named(tallies, offset_by):
        used = int((tallies > 0).sum())
        fixed = max(1, used // 4)
        shifted = fixed + (places - fixed + offset_by * (used - fixed)) % max(1, count - fixed)
        return jnp.zeros((count,), jnp.int32).at[sequence[jnp.where(places < fixed, places, shifted)]].set(jnp.asarray(tallies, jnp.int32))

    tallies = jnp.where(number % 4 == 0, named(packed, number // 4), named(ordinary, number - number // 4 - 1))
    mixed = jax.random.permutation(jax.random.fold_in(own, 3), count)
    giver, taker = mixed[0:count // 2 * 2:2], mixed[1:count // 2 * 2:2]
    margin = jnp.minimum(tallies[giver] - 1, bound - tallies[taker]) // 2
    margin = jnp.where((giver == sequence[0]) | (taker == sequence[0]) | (tallies[taker] == 0), 0, jnp.maximum(margin, 0))
    shifted = jax.random.randint(jax.random.fold_in(own, 4), (count // 2,), 0, 1 << 20) % (margin + 1)
    tallies = tallies.at[giver].add(-shifted).at[taker].add(shifted)
    items = jnp.searchsorted(jnp.cumsum(tallies), jnp.arange(rows * top), side="right").astype(jnp.int32)
    listing = items.reshape(top, rows).T
    listing = listing[jax.random.permutation(jax.random.fold_in(own, 1), rows)]
    offset_by = jax.random.randint(jax.random.fold_in(own, 2), (rows, 1), 0, top)
    return jnp.take_along_axis(listing, (jnp.arange(top)[None, :] + offset_by) % top, axis=1)


def shares(number_of, total, most, skew, full):
    loads = [(1 << 20) // math.isqrt(grade ** skew) + 1 for grade in range(1, number_of + 1)]
    largest = most if full else min(most, max(-(-total // number_of), total * loads[0] // sum(loads)))
    least = 1 if total - largest >= number_of - 1 else 0
    given, surplus = [largest] + [least] * (number_of - 1), total - largest - least * (number_of - 1)
    while surplus > 0:
        movable = [i for i in range(1, number_of) if given[i] < largest] or [i for i in range(1, number_of) if given[i] < most]
        whole, budget = sum([loads[i] for i in movable]), surplus
        for i in movable:
            more = min(most - given[i], max(1, budget * loads[i] // whole), surplus)
            given[i] = given[i] + more
            surplus = surplus - more
    return np.array(given)


def normal_values(key, shape, width, limit, split=(), kind=jnp.bfloat16):
    level = shard_levels(key, shape, split, -0.22, 0.18) if split else 1.0
    drawn = jax.random.normal(key, shape, jnp.float32) * width * level
    return jnp.minimum(jnp.maximum(drawn, -limit), limit).astype(kind)


def setup_inputs(seed: int = 0) -> dict:
    keys = jax.random.split(jax.random.key(seed), 13)
    tracers = normal_values(keys[0], (2, LEV, LAT, LON), 1.0, 6.0, ((1, 8), (2, 4)), jnp.float32)
    layer_mass = jnp.clip(jnp.exp(math.log(2.0) - 1.3862944 * jax.random.uniform(keys[1], (LEV, LAT, LON), jnp.float32) ** shard_levels(keys[1], (LEV, LAT, LON), ((0, 8), (1, 4)), -0.2, 0.2)), 0.5, 2.0)
    courant = jnp.clip(0.1 + 0.79999997 * jax.random.uniform(keys[2], (LEV, LAT), jnp.float32) ** shard_levels(keys[2], (LEV, LAT), ((0, 8), (1, 4)), -0.2, 0.2), 0.1, 0.9)
    remap = draw_remap(jax.random.fold_in(keys[12], 71), 0)
    cost_class = with_ends(jax.random.randint(keys[4], (LAT, LON), 0, 3), jax.random.fold_in(keys[4], 1), 0, 2).astype(jnp.int32)
    spans_keys = jax.random.split(jax.random.fold_in(keys[5], 1), NBLK // BLOCKS_DEV)
    spans_turns = jax.random.permutation(jax.random.fold_in(keys[5], 3), NBLK // BLOCKS_DEV)
    spans = jax.vmap(lambda own, number: shared_out(jax.random.fold_in(keys[5], 2), own, number, BLOCKS_DEV, N_LAT, 1, MOST, 2))(spans_keys, spans_turns).reshape((NBLK, 1))
    w_up = normal_values(keys[6], (EXPERTS, F, HID), F ** -0.5, 0.375, ((0, 4),))
    b_up = normal_values(keys[7], (EXPERTS, HID), 1.0, 6.0, ((0, 4),), jnp.float32)
    w_mid = normal_values(keys[8], (EXPERTS, HID, HID), HID ** -0.5, 0.25, ((0, 4),))
    w_down = normal_values(keys[9], (EXPERTS, HID, F), HID ** -0.5, 0.25, ((0, 4),))
    sw_up = normal_values(keys[10], (EXPERTS, F, HID), F ** -0.5, 0.375, ((0, 4),))
    sw_down = normal_values(keys[11], (EXPERTS, HID, F), HID ** -0.5, 0.25, ((0, 4),))
    return dict(tracers=tracers, layer_mass=layer_mass, courant=courant, remap=remap, cost_class=cost_class, spans=spans, w_up=w_up, b_up=b_up, w_mid=w_mid, w_down=w_down, sw_up=sw_up, sw_down=sw_down)


def minmod(first, second):
    return 0.5 * (jnp.sign(first) + jnp.sign(second)) * jnp.minimum(jnp.abs(first), jnp.abs(second))


def advect(fields, speeds):
    for substep in range(SUBSTEPS):
        east_cell = jnp.roll(fields, -1, axis=-1)
        west_cell = jnp.roll(fields, 1, axis=-1)
        slopes = minmod(east_cell - fields, fields - west_cell)
        fluxes = speeds * (fields + 0.5 * (1.0 - speeds) * slopes)
        fields = fields - (fluxes - jnp.roll(fluxes, 1, axis=-1))
    return fields


def remap_levels(remap, fields):
    masses = jnp.einsum('kl,flyx->fkyx', remap, fields, precision=lax.Precision.HIGHEST)
    return masses[1:] / masses[0]


def physics(features, layer_up, bias_up, layer_mid, layer_down, short_up, short_down):
    hidden = jax.nn.silu(jnp.dot(features, layer_up, preferred_element_type=jnp.float32) + bias_up).astype(jnp.bfloat16)
    deeper = jax.nn.silu(jnp.dot(hidden, layer_mid, preferred_element_type=jnp.float32)).astype(jnp.bfloat16)
    main_out = jnp.dot(deeper, layer_down, preferred_element_type=jnp.float32)
    shortwave = jax.nn.silu(jnp.dot(features, short_up, preferred_element_type=jnp.float32)).astype(jnp.bfloat16)
    side_out = jnp.dot(shortwave, short_down, preferred_element_type=jnp.float32)
    return main_out, side_out


def reference(tracers, layer_mass, courant, remap, cost_class, spans, w_up, b_up, w_mid, w_down, sw_up, sw_down):
    fields = jnp.concatenate([layer_mass[None], tracers * layer_mass[None]], axis=0)
    fields = advect(fields, courant[None, :, :, None])
    mixing = remap_levels(remap, fields)
    features = mixing.reshape(2, LEV, N_LAT, LAT_DEV, N_LEV, LON_DEV).transpose(2, 4, 3, 5, 0, 1)
    features = features.reshape(NBLK, BLK, 2 * LEV).astype(jnp.bfloat16)
    factor = (cost_class.astype(jnp.float32) * 0.5).reshape(N_LAT, LAT_DEV, N_LEV, LON_DEV)
    factor = factor.transpose(0, 2, 1, 3).reshape(NBLK, BLK)

    def one_block(block_item):
        block_rows, expert, block_factor = block_item
        main_out, side_out = physics(block_rows, w_up[expert], b_up[expert], w_mid[expert], w_down[expert], sw_up[expert], sw_down[expert])
        return (main_out + block_factor[:, None] * side_out).astype(jnp.bfloat16)

    tendency = lax.map(one_block, (features, spans[:, 0], factor))
    tendency = tendency.reshape(N_LAT, N_LEV, LAT_DEV, LON_DEV, 2, LEV).transpose(4, 5, 0, 2, 1, 3)
    tendency = tendency.reshape(2, LEV, LAT, LON)
    return mixing + tendency.astype(jnp.float32)
```

```python
import functools

import jax
import jax.numpy as jnp
from jax import lax
from jax.experimental import pallas as pl
from jax.experimental.pallas import tpu as pltpu
from jax.sharding import PartitionSpec as P

LEV = 128
SUBSTEPS = 4
BLK = 16


def minmod(first, second):
    return 0.5 * (jnp.sign(first) + jnp.sign(second)) * jnp.minimum(jnp.abs(first), jnp.abs(second))


def advect(fields, speeds):
    for substep in range(SUBSTEPS):
        east_cell = jnp.roll(fields, -1, axis=-1)
        west_cell = jnp.roll(fields, 1, axis=-1)
        slopes = minmod(east_cell - fields, fields - west_cell)
        fluxes = speeds * (fields + 0.5 * (1.0 - speeds) * slopes)
        fields = fields - (fluxes - jnp.roll(fluxes, 1, axis=-1))
    return fields


def remap_levels(remap, fields):
    masses = jnp.einsum("kl,flyx->fkyx", remap, fields, precision=lax.Precision.HIGHEST)
    return masses[1:] / masses[0]


def physics(features, layer_up, bias_up, layer_mid, layer_down, short_up, short_down):
    hidden = jax.nn.silu(
        jnp.dot(features, layer_up, preferred_element_type=jnp.float32) + bias_up
    ).astype(jnp.bfloat16)
    deeper = jax.nn.silu(jnp.dot(hidden, layer_mid, preferred_element_type=jnp.float32)).astype(
        jnp.bfloat16
    )
    main_out = jnp.dot(deeper, layer_down, preferred_element_type=jnp.float32)
    shortwave = jax.nn.silu(jnp.dot(features, short_up, preferred_element_type=jnp.float32)).astype(
        jnp.bfloat16
    )
    side_out = jnp.dot(shortwave, short_down, preferred_element_type=jnp.float32)
    return (main_out, side_out)


def shards_plain(
    tracers,
    layer_mass,
    courant,
    remap,
    cost_class,
    spans,
    w_up,
    b_up,
    w_mid,
    w_down,
    sw_up,
    sw_down,
):
    fields = jnp.concatenate([layer_mass[None], tracers * layer_mass[None]], axis=0)
    fields = advect(fields, courant[None, :, :, None])
    regrouped = lax.all_to_all(fields, "lev", split_axis=3, concat_axis=1, tiled=True)
    mixing = remap_levels(remap, regrouped)
    width = mixing.shape[2] * mixing.shape[3]
    n_blocks = width // BLK
    groups = lax.axis_size("lat")
    most_blocks = max(2, (n_blocks + groups - 1) // groups)
    slots = groups * most_blocks
    features = mixing.reshape(2 * LEV, width).T.astype(jnp.bfloat16)
    column_blocks = features.reshape(n_blocks, BLK * 2 * LEV)
    factor = cost_class.astype(jnp.float32) * 0.5
    target = spans[:, 0]
    positions = jnp.arange(n_blocks, dtype=jnp.int32)
    earlier = positions[:, None] > positions[None, :]
    same_net = target[:, None] == target[None, :]
    slot_rank = jnp.sum((earlier & same_net).astype(jnp.int32), axis=1)
    slot_id = target * most_blocks + slot_rank
    placing = (jnp.arange(slots, dtype=jnp.int32)[:, None] == slot_id[None, :]).astype(jnp.float32)
    outgoing = jnp.dot(
        placing.astype(jnp.bfloat16), column_blocks, preferred_element_type=jnp.float32
    )
    outgoing = outgoing.astype(jnp.bfloat16).reshape(groups, most_blocks * BLK, 2 * LEV)
    sent_factor = (
        jnp.dot(placing, factor, precision=lax.Precision.HIGHEST)
        .astype(jnp.bfloat16)
        .reshape(groups, most_blocks * BLK)
    )
    incoming, incoming_factor = (
        lax.all_to_all(outgoing, "lat", split_axis=0, concat_axis=0, tiled=True),
        lax.all_to_all(sent_factor, "lat", split_axis=0, concat_axis=0, tiled=True),
    )
    main_out, side_out = physics(
        incoming.reshape(slots * BLK, 2 * LEV),
        w_up[0],
        b_up[0],
        w_mid[0],
        w_down[0],
        sw_up[0],
        sw_down[0],
    )
    owner_sum = (
        main_out + incoming_factor.reshape(slots * BLK).astype(jnp.float32)[:, None] * side_out
    ).astype(jnp.bfloat16)
    returned = lax.all_to_all(
        owner_sum.reshape(groups, most_blocks * BLK, 2 * LEV),
        "lat",
        split_axis=0,
        concat_axis=0,
        tiled=True,
    )
    tendency = jnp.dot(
        placing.T.astype(jnp.bfloat16),
        returned.reshape(slots, BLK * 2 * LEV),
        preferred_element_type=jnp.float32,
    )
    tendency = tendency.astype(jnp.bfloat16).reshape(width, 2 * LEV)
    update = tendency.astype(jnp.float32).T.reshape(mixing.shape)
    return mixing + update


MESH = pl.DeviceIdType.MESH
LANES = 128
SUBLANES = 8
PACK = 16


def as_columns(rows):
    count, width = rows.shape
    shape = (width, width)
    on_diagonal = lax.broadcasted_iota(jnp.int32, shape, 0) == lax.broadcasted_iota(
        jnp.int32, shape, 1
    )
    return [
        jnp.sum(
            jnp.where(on_diagonal, jnp.broadcast_to(rows[i : i + 1, :], shape), 0.0),
            axis=1,
            keepdims=True,
        )
        for i in range(count)
    ]


def transport(fields, speeds):
    weight = 0.5 * speeds * (1.0 - speeds)
    for substep in range(SUBSTEPS):
        ahead = pltpu.roll(fields, LANES - 1, 1) - fields
        behind = pltpu.roll(ahead, 1, 1)
        slopes = jnp.maximum(jnp.minimum(ahead, behind), 0.0) + jnp.minimum(
            jnp.maximum(ahead, behind), 0.0
        )
        fluxes = speeds * fields + weight * slopes
        fields = fields - (fluxes - pltpu.roll(fluxes, 1, 1))
    return fields


def swap_groups(block, width):
    rows = block.shape[0]
    group = lax.broadcasted_iota(jnp.int32, (1, 1, LANES), 2) // width
    block = pltpu.roll(block, 0, 1, stride=width, stride_axis=0)
    block = block.reshape(rows // SUBLANES, SUBLANES, LANES)
    for bit in (1, 2, 4):
        moved = pltpu.roll(block, SUBLANES - bit, 1)
        block = jnp.where((group // bit) % 2 == 1, moved, block)
    block = block.reshape(rows, LANES)
    return pltpu.roll(block, 0, 1, stride=width, stride_axis=0)


def silu(v):
    half = 0.5 * v
    return half + half * jnp.tanh(half)


def step_kernel(
    groups,
    peers,
    most,
    tracers,
    layer_mass,
    courant,
    remap,
    cost_class,
    spans,
    b_up,
    w_up,
    w_mid,
    w_down,
    sw_up,
    sw_down,
    out,
    v_up,
    v_mid,
    v_down,
    v_sup,
    v_sdown,
    turned,
    packed,
    gathered,
    factor_out,
    factor_in,
    columns_out,
    columns_in,
    result_out,
    result_in,
    weight_sems,
    own_sems,
    lev_send,
    lev_recv,
    lat_send,
    lat_recv,
):
    levels, lats, _ = layer_mass.shape
    me, home = lax.axis_index("lev"), lax.axis_index("lat")
    width = LANES // peers
    n_columns = lats * width
    n_blocks = n_columns // BLK
    rows = most * BLK

    barrier = pltpu.get_barrier_semaphore()
    for o in range(1, peers):
        pl.semaphore_signal(
            barrier, inc=1, device_id={"lev": lax.rem(me + o, peers)}, device_id_type=MESH
        )
    for o in range(1, groups):
        pl.semaphore_signal(
            barrier, inc=1, device_id={"lat": lax.rem(home + o, groups)}, device_id_type=MESH
        )
    weights = [
        pltpu.make_async_copy(source, held, weight_sems.at[i])
        for i, (source, held) in enumerate(
            ((w_up, v_up), (sw_up, v_sup), (w_mid, v_mid), (w_down, v_down), (sw_down, v_sdown))
        )
    ]
    for copy in weights:
        copy.start()

    def exchange(stage, source, landing):
        copies = []
        for o in range(1, groups):
            to = lax.rem(home + o, groups)
            copies.append(
                pltpu.make_async_remote_copy(
                    src_ref=source.at[to],
                    dst_ref=landing.at[home],
                    send_sem=lat_send.at[stage, o - 1],
                    recv_sem=lat_recv.at[stage, o - 1],
                    device_id={"lat": to},
                    device_id_type=MESH,
                )
            )
        own = pltpu.make_async_copy(source.at[home], landing.at[home], own_sems.at[stage])
        for copy in copies:
            copy.start()
        own.start()
        return own, copies

    named = [spans[b, 0] for b in range(n_blocks)]
    slot = []
    for b in range(n_blocks):
        rank = jnp.int32(0)
        for earlier in range(b):
            rank = rank + (named[earlier] == named[b]).astype(jnp.int32)
        slot.append((named[b] * most + rank) * BLK)
    lane = lax.broadcasted_iota(jnp.int32, (1, n_columns), 1)
    row_of = jnp.zeros((1, n_columns), jnp.int32)
    for b in range(n_blocks):
        row_of = jnp.where(lane // BLK == b, slot[b], row_of)
    row_of = row_of + lane % BLK
    spread = (groups * rows, n_columns)
    placing = jnp.where(lax.broadcasted_iota(jnp.int32, spread, 0) == row_of, 1.0, 0.0).astype(
        jnp.bfloat16
    )
    day = jnp.concatenate(
        [
            jnp.broadcast_to(column, (width, LANES))
            for column in as_columns(cost_class[...].astype(jnp.float32) * 0.5)
        ],
        axis=0,
    ).astype(jnp.bfloat16)
    factor_out[...] = (
        jnp.dot(placing, day, preferred_element_type=jnp.float32)
        .astype(jnp.bfloat16)
        .reshape(factor_out.shape)
    )

    speeds = as_columns(courant[...])
    chunk = 4
    for first in range(0, levels, chunk):
        speed = jnp.concatenate(
            [jnp.broadcast_to(speeds[first + i], (lats, LANES)) for i in range(chunk)], axis=0
        )
        mass = layer_mass[first : first + chunk].reshape(chunk * lats, LANES)
        for f in range(3):
            field = mass
            if f:
                field = tracers[f - 1, first : first + chunk].reshape(chunk * lats, LANES) * mass
            field = swap_groups(transport(field, speed), width)
            field = field.reshape(chunk, lats // SUBLANES, SUBLANES, LANES)
            for half in range(lats // SUBLANES):
                turned[f, half, first * SUBLANES : (first + chunk) * SUBLANES, :] = field[
                    :, half
                ].reshape(chunk * SUBLANES, LANES)
    for d in range(peers):
        for f in range(3):
            for half in range(lats // SUBLANES):
                packed[
                    d, f * levels : (f + 1) * levels, half * LANES : (half + 1) * LANES
                ] = turned[f, half, pl.ds(d, levels, stride=SUBLANES), :].astype(jnp.bfloat16)

    pl.semaphore_wait(barrier, peers - 1 + groups - 1)
    over_lev = []
    for o in range(1, peers):
        to = lax.rem(me + o, peers)
        over_lev.append(
            pltpu.make_async_remote_copy(
                src_ref=packed.at[lax.rem(peers - to, peers)],
                dst_ref=gathered.at[me],
                send_sem=lev_send.at[o - 1],
                recv_sem=lev_recv.at[o - 1],
                device_id={"lev": to},
                device_id_type=MESH,
            )
        )
        over_lev[-1].start()
    own_lev = pltpu.make_async_copy(
        packed.at[lax.rem(peers - me, peers)], gathered.at[me], own_sems.at[3]
    )
    own_lev.start()
    own_factor, over_factor = exchange(0, factor_out, factor_in)
    own_lev.wait()
    for copy in over_lev:
        copy.wait_recv()

    weight = remap[...].astype(jnp.bfloat16)
    target = [
        jnp.dot(
            weight,
            gathered[:, f * levels : (f + 1) * levels, :].reshape(peers * levels, n_columns),
            preferred_element_type=jnp.float32,
        )
        for f in range(3)
    ]
    inverse = 1.0 / target[0]
    mixing = jnp.concatenate([target[1] * inverse, target[2] * inverse], axis=0)
    columns_out[...] = (
        lax.dot_general(
            placing,
            mixing.astype(jnp.bfloat16),
            (((1,), (1,)), ((), ())),
            preferred_element_type=jnp.float32,
        )
        .astype(jnp.bfloat16)
        .reshape(columns_out.shape)
    )
    own_columns, over_columns = exchange(1, columns_out, columns_in)
    out[...] = mixing
    own_factor.wait()
    for copy in over_factor:
        copy.wait_recv()
    for copy in weights:
        copy.wait()
    own_columns.wait()
    for copy in over_columns:
        copy.wait_recv()

    def dot(a, b):
        return jnp.dot(a, b[0], preferred_element_type=jnp.float32)

    features = columns_in[...].reshape(groups * rows, mixing.shape[0])
    hidden = silu(dot(features, v_up) + b_up[...]).astype(jnp.bfloat16)
    shortwave = silu(dot(features, v_sup)).astype(jnp.bfloat16)
    deeper = silu(dot(hidden, v_mid)).astype(jnp.bfloat16)
    scale = factor_in[...].reshape(groups * rows, LANES).astype(jnp.float32)
    scale = jnp.concatenate([scale] * (mixing.shape[0] // LANES), axis=1)
    result = dot(deeper, v_down) + scale * dot(shortwave, v_sdown)
    result_out[...] = result.astype(jnp.bfloat16).reshape(result_out.shape)
    own_result, over_result = exchange(2, result_out, result_in)
    own_result.wait()
    for copy in over_result:
        copy.wait_recv()
    update = lax.dot_general(
        result_in[...].reshape(groups * rows, mixing.shape[0]),
        placing,
        (((0,), (0,)), ((), ())),
        preferred_element_type=jnp.float32,
    )
    out[...] = out[...] + update
    for copy in over_lev + over_factor + over_columns + over_result:
        copy.wait_send()


def shards_kernel(groups, peers, tracers, layer_mass, courant, remap, cost_class, spans, w_up, b_up, w_mid, w_down, sw_up, sw_down):
    levels, lats, lons = layer_mass.shape
    width = lons // peers
    n_columns = lats * width
    n_blocks = n_columns // BLK
    most = max(2, (n_blocks + groups - 1) // groups)
    rows = most * BLK
    n_features = 2 * levels * peers
    bf16 = jnp.bfloat16
    vmem = pl.BlockSpec(memory_space=pltpu.VMEM)
    hbm = pl.BlockSpec(memory_space=pl.ANY)
    out = pl.pallas_call(
        functools.partial(step_kernel, groups, peers, most),
        out_shape=jax.ShapeDtypeStruct((n_features, n_columns), jnp.float32),
        in_specs=[vmem] * 5 + [pl.BlockSpec(memory_space=pltpu.SMEM), vmem] + [hbm] * 5,
        out_specs=vmem,
        scratch_shapes=[
            pltpu.VMEM(w_up.shape, bf16),
            pltpu.VMEM(w_mid.shape, bf16),
            pltpu.VMEM(w_down.shape, bf16),
            pltpu.VMEM(sw_up.shape, bf16),
            pltpu.VMEM(sw_down.shape, bf16),
            pltpu.VMEM((3, lats // SUBLANES, levels * SUBLANES, LANES), jnp.float32),
            pltpu.VMEM((peers, 3 * levels, n_columns), bf16),
            pltpu.VMEM((peers, 3 * levels, n_columns), bf16),
            pltpu.VMEM((groups, rows, LANES), bf16),
            pltpu.VMEM((groups, rows, LANES), bf16),
            pltpu.VMEM((groups, rows, n_features), bf16),
            pltpu.VMEM((groups, rows, n_features), bf16),
            pltpu.VMEM((groups, rows, n_features), bf16),
            pltpu.VMEM((groups, rows, n_features), bf16),
            pltpu.SemaphoreType.DMA((5,)),
            pltpu.SemaphoreType.DMA((4,)),
            pltpu.SemaphoreType.DMA((peers - 1,)),
            pltpu.SemaphoreType.DMA((peers - 1,)),
            pltpu.SemaphoreType.DMA((3, groups - 1)),
            pltpu.SemaphoreType.DMA((3, groups - 1)),
        ],
        compiler_params=pltpu.CompilerParams(collective_id=0, has_side_effects=True),
    )(tracers, layer_mass, courant, remap, cost_class, spans, b_up, w_up, w_mid, w_down, sw_up, sw_down)
    return out.reshape(2, levels * peers, lats, width)


def shards(groups, peers, *args):
    levels, lats, lons = args[1].shape
    fits = (
        lons == LANES
        and peers == SUBLANES
        and levels % PACK == 0
        and lats % PACK == 0
        and lons // peers == BLK
    )
    return shards_kernel(groups, peers, *args) if fits else shards_plain(*args)


def solution(mesh):
    placed = (
        P(None, "lev", "lat", None),
        P("lev", "lat", None),
        P("lev", "lat"),
        P(),
        P("lat", "lev"),
        P(("lat", "lev"), None),
        P("lat", None, None),
        P("lat", None),
        P("lat", None, None),
        P("lat", None, None),
        P("lat", None, None),
        P("lat", None, None),
    )
    return jax.shard_map(
        functools.partial(shards, mesh.shape["lat"], mesh.shape["lev"]), mesh=mesh, in_specs=placed, out_specs=P(None, None, "lat", "lev"), check_vma=False
    )
```

```python
import functools

import jax
import jax.numpy as jnp
from jax import lax
from jax.experimental import pallas as pl
from jax.experimental.pallas import tpu as pltpu
from jax.sharding import PartitionSpec as P

LEV = 128
SUBSTEPS = 4
BLK = 16


def minmod(first, second):
    return 0.5 * (jnp.sign(first) + jnp.sign(second)) * jnp.minimum(jnp.abs(first), jnp.abs(second))


def advect(fields, speeds):
    for substep in range(SUBSTEPS):
        east_cell = jnp.roll(fields, -1, axis=-1)
        west_cell = jnp.roll(fields, 1, axis=-1)
        slopes = minmod(east_cell - fields, fields - west_cell)
        fluxes = speeds * (fields + 0.5 * (1.0 - speeds) * slopes)
        fields = fields - (fluxes - jnp.roll(fluxes, 1, axis=-1))
    return fields


def remap_levels(remap, fields):
    masses = jnp.einsum("kl,flyx->fkyx", remap, fields, precision=lax.Precision.HIGHEST)
    return masses[1:] / masses[0]


def physics(features, layer_up, bias_up, layer_mid, layer_down, short_up, short_down):
    hidden = jax.nn.silu(
        jnp.dot(features, layer_up, preferred_element_type=jnp.float32) + bias_up
    ).astype(jnp.bfloat16)
    deeper = jax.nn.silu(jnp.dot(hidden, layer_mid, preferred_element_type=jnp.float32)).astype(
        jnp.bfloat16
    )
    main_out = jnp.dot(deeper, layer_down, preferred_element_type=jnp.float32)
    shortwave = jax.nn.silu(jnp.dot(features, short_up, preferred_element_type=jnp.float32)).astype(
        jnp.bfloat16
    )
    side_out = jnp.dot(shortwave, short_down, preferred_element_type=jnp.float32)
    return (main_out, side_out)


def shards_plain(
    tracers,
    layer_mass,
    courant,
    remap,
    cost_class,
    spans,
    w_up,
    b_up,
    w_mid,
    w_down,
    sw_up,
    sw_down,
):
    fields = jnp.concatenate([layer_mass[None], tracers * layer_mass[None]], axis=0)
    fields = advect(fields, courant[None, :, :, None])
    regrouped = lax.all_to_all(fields, "lev", split_axis=3, concat_axis=1, tiled=True)
    mixing = remap_levels(remap, regrouped)
    width = mixing.shape[2] * mixing.shape[3]
    n_blocks = width // BLK
    groups = lax.axis_size("lat")
    most_blocks = max(2, (n_blocks + groups - 1) // groups)
    slots = groups * most_blocks
    features = mixing.reshape(2 * LEV, width).T.astype(jnp.bfloat16)
    column_blocks = features.reshape(n_blocks, BLK * 2 * LEV)
    factor = cost_class.astype(jnp.float32) * 0.5
    target = spans[:, 0]
    positions = jnp.arange(n_blocks, dtype=jnp.int32)
    earlier = positions[:, None] > positions[None, :]
    same_net = target[:, None] == target[None, :]
    slot_rank = jnp.sum((earlier & same_net).astype(jnp.int32), axis=1)
    slot_id = target * most_blocks + slot_rank
    placing = (jnp.arange(slots, dtype=jnp.int32)[:, None] == slot_id[None, :]).astype(jnp.float32)
    outgoing = jnp.dot(
        placing.astype(jnp.bfloat16), column_blocks, preferred_element_type=jnp.float32
    )
    outgoing = outgoing.astype(jnp.bfloat16).reshape(groups, most_blocks * BLK, 2 * LEV)
    sent_factor = (
        jnp.dot(placing, factor, precision=lax.Precision.HIGHEST)
        .astype(jnp.bfloat16)
        .reshape(groups, most_blocks * BLK)
    )
    incoming, incoming_factor = (
        lax.all_to_all(outgoing, "lat", split_axis=0, concat_axis=0, tiled=True),
        lax.all_to_all(sent_factor, "lat", split_axis=0, concat_axis=0, tiled=True),
    )
    main_out, side_out = physics(
        incoming.reshape(slots * BLK, 2 * LEV),
        w_up[0],
        b_up[0],
        w_mid[0],
        w_down[0],
        sw_up[0],
        sw_down[0],
    )
    owner_sum = (
        main_out + incoming_factor.reshape(slots * BLK).astype(jnp.float32)[:, None] * side_out
    ).astype(jnp.bfloat16)
    returned = lax.all_to_all(
        owner_sum.reshape(groups, most_blocks * BLK, 2 * LEV),
        "lat",
        split_axis=0,
        concat_axis=0,
        tiled=True,
    )
    tendency = jnp.dot(
        placing.T.astype(jnp.bfloat16),
        returned.reshape(slots, BLK * 2 * LEV),
        preferred_element_type=jnp.float32,
    )
    tendency = tendency.astype(jnp.bfloat16).reshape(width, 2 * LEV)
    update = tendency.astype(jnp.float32).T.reshape(mixing.shape)
    return mixing + update


MESH = pl.DeviceIdType.MESH
LANES = 128
SUBLANES = 8
PACK = 16


def as_columns(rows):
    count, width = rows.shape
    shape = (width, width)
    on_diagonal = lax.broadcasted_iota(jnp.int32, shape, 0) == lax.broadcasted_iota(
        jnp.int32, shape, 1
    )
    return [
        jnp.sum(
            jnp.where(on_diagonal, jnp.broadcast_to(rows[i : i + 1, :], shape), 0.0),
            axis=1,
            keepdims=True,
        )
        for i in range(count)
    ]


def transport(fields, speeds):
    weight = 0.5 * speeds * (1.0 - speeds)
    for substep in range(SUBSTEPS):
        ahead = pltpu.roll(fields, LANES - 1, 1) - fields
        behind = fields - pltpu.roll(fields, 1, 1)
        slopes = jnp.maximum(jnp.minimum(ahead, behind), 0.0) + jnp.minimum(
            jnp.maximum(ahead, behind), 0.0
        )
        fluxes = speeds * fields + weight * slopes
        fields = fields - (fluxes - pltpu.roll(fluxes, 1, 1))
    return fields


def swap_groups(block, width):
    rows = block.shape[0]
    group = lax.broadcasted_iota(jnp.int32, (1, 1, LANES), 2) // width
    block = pltpu.roll(block, 0, 1, stride=width, stride_axis=0)
    block = block.reshape(rows // SUBLANES, SUBLANES, LANES)
    for bit in (1, 2, 4):
        moved = pltpu.roll(block, SUBLANES - bit, 1)
        block = jnp.where((group // bit) % 2 == 1, moved, block)
    block = block.reshape(rows, LANES)
    return pltpu.roll(block, 0, 1, stride=width, stride_axis=0)


def silu(v):
    half = 0.5 * v
    return half + half * jnp.tanh(half)


def step_kernel(
    groups,
    peers,
    most,
    tracers,
    layer_mass,
    courant,
    remap,
    cost_class,
    spans,
    b_up,
    w_up,
    w_mid,
    w_down,
    sw_up,
    sw_down,
    out,
    v_up,
    v_mid,
    v_down,
    v_sup,
    v_sdown,
    turned,
    packed,
    gathered,
    factor_out,
    factor_in,
    columns_out,
    columns_in,
    result_out,
    result_in,
    weight_sems,
    own_sems,
    lev_send,
    lev_recv,
    lat_send,
    lat_recv,
):
    levels, lats, _ = layer_mass.shape
    me, home = lax.axis_index("lev"), lax.axis_index("lat")
    width = LANES // peers
    n_columns = lats * width
    n_blocks = n_columns // BLK
    rows = most * BLK

    barrier = pltpu.get_barrier_semaphore()
    for o in range(1, peers):
        pl.semaphore_signal(
            barrier, inc=1, device_id={"lev": lax.rem(me + o, peers)}, device_id_type=MESH
        )
    for o in range(1, groups):
        pl.semaphore_signal(
            barrier, inc=1, device_id={"lat": lax.rem(home + o, groups)}, device_id_type=MESH
        )
    weights = [
        pltpu.make_async_copy(source, held, weight_sems.at[i])
        for i, (source, held) in enumerate(
            ((w_up, v_up), (sw_up, v_sup), (w_mid, v_mid), (w_down, v_down), (sw_down, v_sdown))
        )
    ]
    for copy in weights:
        copy.start()

    def exchange(stage, source, landing):
        copies = []
        for o in range(1, groups):
            to = lax.rem(home + o, groups)
            copies.append(
                pltpu.make_async_remote_copy(
                    src_ref=source.at[to],
                    dst_ref=landing.at[home],
                    send_sem=lat_send.at[stage, o - 1],
                    recv_sem=lat_recv.at[stage, o - 1],
                    device_id={"lat": to},
                    device_id_type=MESH,
                )
            )
        own = pltpu.make_async_copy(source.at[home], landing.at[home], own_sems.at[stage])
        for copy in copies:
            copy.start()
        own.start()
        return own, copies

    named = [spans[0, b] for b in range(n_blocks)]
    slot = []
    for b in range(n_blocks):
        rank = jnp.int32(0)
        for earlier in range(b):
            rank = rank + (named[earlier] == named[b]).astype(jnp.int32)
        slot.append((named[b] * most + rank) * BLK)
    lane = lax.broadcasted_iota(jnp.int32, (1, n_columns), 1)
    row_of = jnp.zeros((1, n_columns), jnp.int32)
    for b in range(n_blocks):
        row_of = jnp.where(lane // BLK == b, slot[b], row_of)
    row_of = row_of + lane % BLK
    spread = (groups * rows, n_columns)
    placing = jnp.where(lax.broadcasted_iota(jnp.int32, spread, 0) == row_of, 1.0, 0.0).astype(
        jnp.bfloat16
    )
    offset = lax.broadcasted_iota(jnp.int32, (BLK, groups * rows), 1) - lax.broadcasted_iota(
        jnp.int32, (BLK, groups * rows), 0
    )
    restoring = jnp.concatenate(
        [jnp.where(offset == slot[b], 1.0, 0.0) for b in range(n_blocks)], axis=0
    ).astype(jnp.bfloat16)
    day = jnp.concatenate(
        [
            jnp.broadcast_to(column, (width, LANES))
            for column in as_columns(cost_class[...].astype(jnp.float32) * 0.5)
        ],
        axis=0,
    ).astype(jnp.bfloat16)
    factor_out[...] = (
        jnp.dot(placing, day, preferred_element_type=jnp.float32)
        .astype(jnp.bfloat16)
        .reshape(factor_out.shape)
    )

    speed = jnp.concatenate(
        [jnp.broadcast_to(column, (lats, LANES)) for column in as_columns(courant[...])], axis=0
    )
    mass = layer_mass[...].reshape(levels * lats, LANES)
    side = me // (peers // 2)
    others = []
    for k in range(peers - 1):
        low = peers - 1 - k
        low = low - (low <= me).astype(jnp.int32)
        high = k + (k >= me).astype(jnp.int32)
        others.append(side * high + (1 - side) * low)
    over_lev = []
    for f in range(3):
        field = mass
        if f:
            field = tracers[f - 1].reshape(levels * lats, LANES) * mass
        field = swap_groups(transport(field, speed), width)
        field = field.reshape(levels, lats // SUBLANES, SUBLANES, LANES)
        for half in range(lats // SUBLANES):
            turned[f, half] = field[:, half].reshape(levels * SUBLANES, LANES)
        for d in range(peers):
            for half in range(lats // SUBLANES):
                packed[f, d, :, half * LANES : (half + 1) * LANES] = turned[
                    f, half, pl.ds(d, levels, stride=SUBLANES), :
                ].astype(jnp.bfloat16)
        if f == 0:
            pl.semaphore_wait(barrier, peers - 1 + groups - 1)
        copies = []
        for k, to in enumerate(others):
            copy = pltpu.make_async_remote_copy(
                src_ref=packed.at[f, lax.rem(peers - to, peers)],
                dst_ref=gathered.at[f, me],
                send_sem=lev_send.at[f, k],
                recv_sem=lev_recv.at[f, me],
                device_id={"lev": to},
                device_id_type=MESH,
            )
            copy.start()
            copies.append(copy)
        own = pltpu.make_async_copy(
            packed.at[f, lax.rem(peers - me, peers)], gathered.at[f, me], own_sems.at[3 + f]
        )
        own.start()
        over_lev.append((own, copies))
    own_factor, over_factor = exchange(0, factor_out, factor_in)
    weight = remap[...].astype(jnp.bfloat16)
    target = []
    for f in range(3):
        over_lev[f][0].wait()
        for k, source in enumerate(others):
            pltpu.make_async_remote_copy(
                src_ref=packed.at[f, 0],
                dst_ref=gathered.at[f, source],
                send_sem=lev_send.at[f, k],
                recv_sem=lev_recv.at[f, source],
                device_id={"lev": source},
                device_id_type=MESH,
            ).wait_recv()
        target.append(
            lax.dot_general(
                gathered[f].reshape(peers * levels, n_columns),
                weight,
                (((0,), (1,)), ((), ())),
                preferred_element_type=jnp.float32,
            )
        )
    inverse = 1.0 / target[0]
    mixing = jnp.concatenate([target[1] * inverse, target[2] * inverse], axis=1)
    columns_out[...] = (
        jnp.dot(placing, mixing.astype(jnp.bfloat16), preferred_element_type=jnp.float32)
        .astype(jnp.bfloat16)
        .reshape(columns_out.shape)
    )
    own_columns, over_columns = exchange(1, columns_out, columns_in)
    for t in range(2):
        out[t] = mixing[:, t * LANES : (t + 1) * LANES]
    own_factor.wait()
    for copy in over_factor:
        copy.wait_recv()
    for copy in weights:
        copy.wait()
    own_columns.wait()
    for copy in over_columns:
        copy.wait_recv()

    def dot(a, b):
        return jnp.dot(a, b[0], preferred_element_type=jnp.float32)

    features = columns_in[...].reshape(groups * rows, mixing.shape[1])
    hidden = silu(dot(features, v_up) + b_up[...]).astype(jnp.bfloat16)
    shortwave = silu(dot(features, v_sup)).astype(jnp.bfloat16)
    deeper = silu(dot(hidden, v_mid)).astype(jnp.bfloat16)
    scale = factor_in[...].reshape(groups * rows, LANES).astype(jnp.float32)
    scale = jnp.concatenate([scale] * (mixing.shape[1] // LANES), axis=1)
    result = dot(deeper, v_down) + scale * dot(shortwave, v_sdown)
    result_out[...] = result.astype(jnp.bfloat16).reshape(result_out.shape)
    own_result, over_result = exchange(2, result_out, result_in)
    own_result.wait()
    for copy in over_result:
        copy.wait_recv()
    update = jnp.dot(
        restoring,
        result_in[...].reshape(groups * rows, mixing.shape[1]),
        preferred_element_type=jnp.float32,
    )
    for t in range(2):
        out[t] = out[t] + update[:, t * LANES : (t + 1) * LANES]
    for copy in over_factor + over_columns + over_result:
        copy.wait_send()
    for own, copies in over_lev:
        for copy in copies:
            copy.wait_send()


def shards_kernel(groups, peers, tracers, layer_mass, courant, remap, cost_class, spans, w_up, b_up, w_mid, w_down, sw_up, sw_down):
    levels, lats, lons = layer_mass.shape
    width = lons // peers
    n_columns = lats * width
    n_blocks = n_columns // BLK
    most = max(2, (n_blocks + groups - 1) // groups)
    rows = most * BLK
    n_features = 2 * levels * peers
    bf16 = jnp.bfloat16
    vmem = pl.BlockSpec(memory_space=pltpu.VMEM)
    hbm = pl.BlockSpec(memory_space=pl.ANY)
    out = pl.pallas_call(
        functools.partial(step_kernel, groups, peers, most),
        out_shape=jax.ShapeDtypeStruct((2, n_columns, levels * peers), jnp.float32),
        in_specs=[vmem] * 5 + [pl.BlockSpec(memory_space=pltpu.SMEM), vmem] + [hbm] * 5,
        out_specs=vmem,
        scratch_shapes=[
            pltpu.VMEM(w_up.shape, bf16),
            pltpu.VMEM(w_mid.shape, bf16),
            pltpu.VMEM(w_down.shape, bf16),
            pltpu.VMEM(sw_up.shape, bf16),
            pltpu.VMEM(sw_down.shape, bf16),
            pltpu.VMEM((3, lats // SUBLANES, levels * SUBLANES, LANES), jnp.float32),
            pltpu.VMEM((3, peers, levels, n_columns), bf16),
            pltpu.VMEM((3, peers, levels, n_columns), bf16),
            pltpu.VMEM((groups, rows, LANES), bf16),
            pltpu.VMEM((groups, rows, LANES), bf16),
            pltpu.VMEM((groups, rows, n_features), bf16),
            pltpu.VMEM((groups, rows, n_features), bf16),
            pltpu.VMEM((groups, rows, n_features), bf16),
            pltpu.VMEM((groups, rows, n_features), bf16),
            pltpu.SemaphoreType.DMA((5,)),
            pltpu.SemaphoreType.DMA((6,)),
            pltpu.SemaphoreType.DMA((3, peers - 1)),
            pltpu.SemaphoreType.DMA((3, peers)),
            pltpu.SemaphoreType.DMA((3, groups - 1)),
            pltpu.SemaphoreType.DMA((3, groups - 1)),
        ],
        compiler_params=pltpu.CompilerParams(collective_id=0, has_side_effects=True),
    )(tracers, layer_mass, courant, remap, cost_class, spans.reshape(1, -1), b_up, w_up, w_mid, w_down, sw_up, sw_down)
    return out.reshape(2, lats, width, levels * peers).transpose(0, 3, 1, 2)


def shards(groups, peers, *args):
    levels, lats, lons = args[1].shape
    fits = (
        lons == LANES
        and peers == SUBLANES
        and levels % PACK == 0
        and lats % PACK == 0
        and lons // peers == BLK
        and levels * peers == LANES
    )
    return shards_kernel(groups, peers, *args) if fits else shards_plain(*args)


def solution(mesh):
    placed = (
        P(None, "lev", "lat", None),
        P("lev", "lat", None),
        P("lev", "lat"),
        P(),
        P("lat", "lev"),
        P(("lat", "lev"), None),
        P("lat", None, None),
        P("lat", None),
        P("lat", None, None),
        P("lat", None, None),
        P("lat", None, None),
        P("lat", None, None),
    )
    return jax.shard_map(
        functools.partial(shards, mesh.shape["lat"], mesh.shape["lev"]), mesh=mesh, in_specs=placed, out_specs=P(None, None, "lat", "lev"), check_vma=False
    )
```

```python
import functools

import jax
import jax.numpy as jnp
from jax import lax
from jax.experimental import pallas as pl
from jax.experimental.pallas import tpu as pltpu
from jax.sharding import PartitionSpec as P

LEV = 128
SUBSTEPS = 4
BLK = 16


def minmod(first, second):
    return 0.5 * (jnp.sign(first) + jnp.sign(second)) * jnp.minimum(jnp.abs(first), jnp.abs(second))


def advect(fields, speeds):
    for substep in range(SUBSTEPS):
        east_cell = jnp.roll(fields, -1, axis=-1)
        west_cell = jnp.roll(fields, 1, axis=-1)
        slopes = minmod(east_cell - fields, fields - west_cell)
        fluxes = speeds * (fields + 0.5 * (1.0 - speeds) * slopes)
        fields = fields - (fluxes - jnp.roll(fluxes, 1, axis=-1))
    return fields


def remap_levels(remap, fields):
    masses = jnp.einsum("kl,flyx->fkyx", remap, fields, precision=lax.Precision.HIGHEST)
    return masses[1:] / masses[0]


def physics(features, layer_up, bias_up, layer_mid, layer_down, short_up, short_down):
    hidden = jax.nn.silu(
        jnp.dot(features, layer_up, preferred_element_type=jnp.float32) + bias_up
    ).astype(jnp.bfloat16)
    deeper = jax.nn.silu(jnp.dot(hidden, layer_mid, preferred_element_type=jnp.float32)).astype(
        jnp.bfloat16
    )
    main_out = jnp.dot(deeper, layer_down, preferred_element_type=jnp.float32)
    shortwave = jax.nn.silu(jnp.dot(features, short_up, preferred_element_type=jnp.float32)).astype(
        jnp.bfloat16
    )
    side_out = jnp.dot(shortwave, short_down, preferred_element_type=jnp.float32)
    return (main_out, side_out)


def shards_plain(
    tracers,
    layer_mass,
    courant,
    remap,
    cost_class,
    spans,
    w_up,
    b_up,
    w_mid,
    w_down,
    sw_up,
    sw_down,
):
    fields = jnp.concatenate([layer_mass[None], tracers * layer_mass[None]], axis=0)
    fields = advect(fields, courant[None, :, :, None])
    regrouped = lax.all_to_all(fields, "lev", split_axis=3, concat_axis=1, tiled=True)
    mixing = remap_levels(remap, regrouped)
    width = mixing.shape[2] * mixing.shape[3]
    n_blocks = width // BLK
    groups = lax.axis_size("lat")
    most_blocks = max(2, (n_blocks + groups - 1) // groups)
    slots = groups * most_blocks
    features = mixing.reshape(2 * LEV, width).T.astype(jnp.bfloat16)
    column_blocks = features.reshape(n_blocks, BLK * 2 * LEV)
    factor = cost_class.astype(jnp.float32) * 0.5
    target = spans[:, 0]
    positions = jnp.arange(n_blocks, dtype=jnp.int32)
    earlier = positions[:, None] > positions[None, :]
    same_net = target[:, None] == target[None, :]
    slot_rank = jnp.sum((earlier & same_net).astype(jnp.int32), axis=1)
    slot_id = target * most_blocks + slot_rank
    placing = (jnp.arange(slots, dtype=jnp.int32)[:, None] == slot_id[None, :]).astype(jnp.float32)
    outgoing = jnp.dot(
        placing.astype(jnp.bfloat16), column_blocks, preferred_element_type=jnp.float32
    )
    outgoing = outgoing.astype(jnp.bfloat16).reshape(groups, most_blocks * BLK, 2 * LEV)
    sent_factor = (
        jnp.dot(placing, factor, precision=lax.Precision.HIGHEST)
        .astype(jnp.bfloat16)
        .reshape(groups, most_blocks * BLK)
    )
    incoming, incoming_factor = (
        lax.all_to_all(outgoing, "lat", split_axis=0, concat_axis=0, tiled=True),
        lax.all_to_all(sent_factor, "lat", split_axis=0, concat_axis=0, tiled=True),
    )
    main_out, side_out = physics(
        incoming.reshape(slots * BLK, 2 * LEV),
        w_up[0],
        b_up[0],
        w_mid[0],
        w_down[0],
        sw_up[0],
        sw_down[0],
    )
    owner_sum = (
        main_out + incoming_factor.reshape(slots * BLK).astype(jnp.float32)[:, None] * side_out
    ).astype(jnp.bfloat16)
    returned = lax.all_to_all(
        owner_sum.reshape(groups, most_blocks * BLK, 2 * LEV),
        "lat",
        split_axis=0,
        concat_axis=0,
        tiled=True,
    )
    tendency = jnp.dot(
        placing.T.astype(jnp.bfloat16),
        returned.reshape(slots, BLK * 2 * LEV),
        preferred_element_type=jnp.float32,
    )
    tendency = tendency.astype(jnp.bfloat16).reshape(width, 2 * LEV)
    update = tendency.astype(jnp.float32).T.reshape(mixing.shape)
    return mixing + update


MESH = pl.DeviceIdType.MESH
LANES = 128
SUBLANES = 8
PACK = 16


def as_columns(rows):
    count, width = rows.shape
    shape = (width, width)
    on_diagonal = lax.broadcasted_iota(jnp.int32, shape, 0) == lax.broadcasted_iota(
        jnp.int32, shape, 1
    )
    return [
        jnp.sum(
            jnp.where(on_diagonal, jnp.broadcast_to(rows[i : i + 1, :], shape), 0.0),
            axis=1,
            keepdims=True,
        )
        for i in range(count)
    ]


def transport(fields, speeds):
    weight = 0.5 * speeds * (1.0 - speeds)
    for substep in range(SUBSTEPS):
        ahead = pltpu.roll(fields, LANES - 1, 1) - fields
        behind = fields - pltpu.roll(fields, 1, 1)
        slopes = jnp.maximum(jnp.minimum(ahead, behind), 0.0) + jnp.minimum(
            jnp.maximum(ahead, behind), 0.0
        )
        fluxes = speeds * fields + weight * slopes
        fields = fields - (fluxes - pltpu.roll(fluxes, 1, 1))
    return fields


def swap_groups(block, width):
    rows = block.shape[0]
    group = lax.broadcasted_iota(jnp.int32, (1, 1, LANES), 2) // width
    block = pltpu.roll(block, 0, 1, stride=width, stride_axis=0)
    block = block.reshape(rows // SUBLANES, SUBLANES, LANES)
    for bit in (1, 2, 4):
        moved = pltpu.roll(block, SUBLANES - bit, 1)
        block = jnp.where((group // bit) % 2 == 1, moved, block)
    block = block.reshape(rows, LANES)
    return pltpu.roll(block, 0, 1, stride=width, stride_axis=0)


def silu(v):
    half = 0.5 * v
    return half + half * jnp.tanh(half)


def step_kernel(
    groups,
    peers,
    most,
    tracers,
    layer_mass,
    courant,
    remap,
    cost_class,
    spans,
    b_up,
    w_up,
    w_mid,
    w_down,
    sw_up,
    sw_down,
    mixing_out,
    update_out,
    v_up,
    v_mid,
    v_down,
    v_sup,
    v_sdown,
    turned,
    packed,
    gathered,
    factor_out,
    factor_in,
    columns_out,
    columns_in,
    result_out,
    result_in,
    mixed,
    weight_sems,
    own_sems,
    lev_send,
    lev_recv,
    lat_send,
    lat_recv,
):
    levels, lats, _ = layer_mass.shape
    me, home = lax.axis_index("lev"), lax.axis_index("lat")
    width = LANES // peers
    n_columns = lats * width
    n_blocks = n_columns // BLK
    rows = most * BLK

    barrier = pltpu.get_barrier_semaphore()
    for o in range(1, peers):
        pl.semaphore_signal(
            barrier, inc=1, device_id={"lev": lax.rem(me + o, peers)}, device_id_type=MESH
        )
    for o in range(1, groups):
        pl.semaphore_signal(
            barrier, inc=1, device_id={"lat": lax.rem(home + o, groups)}, device_id_type=MESH
        )
    weights = [
        pltpu.make_async_copy(source, held, weight_sems.at[i])
        for i, (source, held) in enumerate(
            ((w_up, v_up), (sw_up, v_sup), (w_mid, v_mid), (w_down, v_down), (sw_down, v_sdown))
        )
    ]
    for copy in weights:
        copy.start()

    speed = jnp.concatenate(
        [jnp.broadcast_to(column, (lats, LANES)) for column in as_columns(courant[...])], axis=0
    )
    mass = layer_mass[...].reshape(levels * lats, LANES)
    side = me // (peers // 2)
    others = []
    for k in range(peers - 1):
        low = peers - 1 - k
        low = low - (low <= me).astype(jnp.int32)
        high = k + (k >= me).astype(jnp.int32)
        others.append(side * high + (1 - side) * low)
    own_lev = []
    for f in range(3):
        field = mass
        if f:
            field = tracers[f - 1].reshape(levels * lats, LANES) * mass
        field = swap_groups(transport(field, speed), width)
        field = field.reshape(levels, lats // SUBLANES, SUBLANES, LANES)
        for half in range(lats // SUBLANES):
            turned[f, half] = field[:, half].reshape(levels * SUBLANES, LANES)
        for d in range(peers):
            for half in range(lats // SUBLANES):
                packed[f, d, :, half * LANES : (half + 1) * LANES] = turned[
                    f, half, pl.ds(d, levels, stride=SUBLANES), :
                ].astype(jnp.bfloat16)
        if f == 0:
            pl.semaphore_wait(barrier, peers - 1 + groups - 1)
        for to in others:
            copy = pltpu.make_async_remote_copy(
                src_ref=packed.at[f, lax.rem(peers - to, peers)],
                dst_ref=gathered.at[f, me],
                send_sem=lev_send,
                recv_sem=lev_recv.at[f],
                device_id={"lev": to},
                device_id_type=MESH,
            )
            copy.start()
        own = pltpu.make_async_copy(
            packed.at[f, lax.rem(peers - me, peers)], gathered.at[f, me], own_sems.at[f]
        )
        own.start()
        own_lev.append(own)
    named = [spans[0, b] for b in range(n_blocks)]
    slot = []
    for b in range(n_blocks):
        rank = jnp.int32(0)
        for earlier in range(b):
            rank = rank + (named[earlier] == named[b]).astype(jnp.int32)
        slot.append((named[b] * most + rank) * BLK)
    lane = lax.broadcasted_iota(jnp.int32, (1, n_columns), 1)
    row_of = jnp.zeros((1, n_columns), jnp.int32)
    for b in range(n_blocks):
        row_of = jnp.where(lane // BLK == b, slot[b], row_of)
    row_of = row_of + lane % BLK
    spread = (groups * rows, n_columns)
    placing = jnp.where(lax.broadcasted_iota(jnp.int32, spread, 0) == row_of, 1.0, 0.0).astype(
        jnp.bfloat16
    )
    offset = lax.broadcasted_iota(jnp.int32, (BLK, groups * rows), 1) - lax.broadcasted_iota(
        jnp.int32, (BLK, groups * rows), 0
    )
    restoring = jnp.concatenate(
        [jnp.where(offset == slot[b], 1.0, 0.0) for b in range(n_blocks)], axis=0
    ).astype(jnp.bfloat16)
    day = jnp.concatenate(
        [
            jnp.broadcast_to(column, (width, LANES))
            for column in as_columns(cost_class[...].astype(jnp.float32) * 0.5)
        ],
        axis=0,
    ).astype(jnp.bfloat16)
    factor_out[...] = (
        jnp.dot(placing, day, preferred_element_type=jnp.float32)
        .astype(jnp.bfloat16)
        .reshape(factor_out.shape)
    )

    turn = 1 - 2 * lax.rem(home, 2)
    partners = [lax.rem(home + turn * o + groups * groups, groups) for o in range(groups - 1, 0, -1)]

    def send(stage, source, landing, arrival, to):
        copy = pltpu.make_async_remote_copy(
            src_ref=source.at[to],
            dst_ref=landing.at[home],
            send_sem=lat_send.at[stage],
            recv_sem=arrival,
            device_id={"lat": to},
            device_id_type=MESH,
        )
        copy.start()

    def all_partners(stage, source, landing, arrival):
        return pltpu.make_async_remote_copy(
            src_ref=source.at[pl.ds(0, groups - 1)],
            dst_ref=landing.at[pl.ds(0, groups - 1)],
            send_sem=lat_send.at[stage],
            recv_sem=arrival,
            device_id={"lat": partners[0]},
            device_id_type=MESH,
        )

    for to in partners:
        send(0, factor_out, factor_in, lat_recv.at[groups], to)
    weight = remap[...].astype(jnp.bfloat16)
    target = []
    for f in range(3):
        own_lev[f].wait()
        pltpu.make_async_remote_copy(
            src_ref=packed.at[f, pl.ds(0, peers - 1)],
            dst_ref=gathered.at[f, pl.ds(0, peers - 1)],
            send_sem=lev_send,
            recv_sem=lev_recv.at[f],
            device_id={"lev": others[0]},
            device_id_type=MESH,
        ).wait_recv()
        target.append(
            lax.dot_general(
                gathered[f].reshape(peers * levels, n_columns),
                weight,
                (((0,), (1,)), ((), ())),
                preferred_element_type=jnp.float32,
            )
        )
    inverse = 1.0 / target[0]
    mixing = jnp.concatenate([target[1] * inverse, target[2] * inverse], axis=1)
    columns_out[...] = (
        jnp.dot(placing, mixing.astype(jnp.bfloat16), preferred_element_type=jnp.float32)
        .astype(jnp.bfloat16)
        .reshape(columns_out.shape)
    )
    for to in partners:
        send(1, columns_out, columns_in, lat_recv.at[home], to)
    for t in range(2):
        mixed[t] = mixing[:, t * LANES : (t + 1) * LANES]
    own_mixed = pltpu.make_async_copy(mixed, mixing_out, own_sems.at[3])
    own_mixed.start()
    for copy in weights:
        copy.wait()

    def dot(a, b):
        return jnp.dot(a, b[0], preferred_element_type=jnp.float32)

    def nets(features, scale):
        hidden = silu(dot(features, v_up) + b_up[...]).astype(jnp.bfloat16)
        shortwave = silu(dot(features, v_sup)).astype(jnp.bfloat16)
        deeper = silu(dot(hidden, v_mid)).astype(jnp.bfloat16)
        scale = jnp.concatenate([scale.astype(jnp.float32)] * (mixing.shape[1] // LANES), axis=1)
        return (dot(deeper, v_down) + scale * dot(shortwave, v_sdown)).astype(jnp.bfloat16)

    result_in[home] = nets(columns_out[home], factor_out[home])
    all_partners(0, factor_out, factor_in, lat_recv.at[groups]).wait_recv()
    for batch in (partners[:1], partners[1:]):
        for source in batch:
            pltpu.make_async_remote_copy(
                src_ref=columns_out.at[source],
                dst_ref=columns_in.at[source],
                send_sem=lat_send.at[1],
                recv_sem=lat_recv.at[source],
                device_id={"lat": source},
                device_id_type=MESH,
            ).wait_recv()
        result = nets(
            jnp.concatenate([columns_in[source] for source in batch], axis=0),
            jnp.concatenate([factor_in[source] for source in batch], axis=0),
        )
        for i, source in enumerate(batch):
            result_out[source] = result[i * rows : (i + 1) * rows]
            send(2, result_out, result_in, lat_recv.at[groups + 1], source)
    all_partners(2, result_out, result_in, lat_recv.at[groups + 1]).wait_recv()
    update = jnp.dot(
        restoring,
        result_in[...].reshape(groups * rows, mixing.shape[1]),
        preferred_element_type=jnp.float32,
    )
    for t in range(2):
        update_out[t] = update[:, t * LANES : (t + 1) * LANES].astype(jnp.bfloat16)
    own_mixed.wait()
    all_partners(0, factor_out, factor_in, lat_recv.at[groups]).wait_send()
    all_partners(1, columns_out, columns_in, lat_recv.at[groups]).wait_send()
    all_partners(2, result_out, result_in, lat_recv.at[groups]).wait_send()
    pltpu.make_async_remote_copy(
        src_ref=packed.at[:, pl.ds(0, peers - 1)],
        dst_ref=gathered.at[:, pl.ds(0, peers - 1)],
        send_sem=lev_send,
        recv_sem=lev_recv.at[0],
        device_id={"lev": others[0]},
        device_id_type=MESH,
    ).wait_send()


def shards_kernel(groups, peers, tracers, layer_mass, courant, remap, cost_class, spans, w_up, b_up, w_mid, w_down, sw_up, sw_down):
    levels, lats, lons = layer_mass.shape
    width = lons // peers
    n_columns = lats * width
    n_blocks = n_columns // BLK
    most = max(2, (n_blocks + groups - 1) // groups)
    rows = most * BLK
    n_features = 2 * levels * peers
    bf16 = jnp.bfloat16
    vmem = pl.BlockSpec(memory_space=pltpu.VMEM)
    hbm = pl.BlockSpec(memory_space=pl.ANY)
    mixing, update = pl.pallas_call(
        functools.partial(step_kernel, groups, peers, most),
        out_shape=(
            jax.ShapeDtypeStruct((2, n_columns, levels * peers), jnp.float32),
            jax.ShapeDtypeStruct((2, n_columns, levels * peers), bf16),
        ),
        in_specs=[vmem] * 5 + [pl.BlockSpec(memory_space=pltpu.SMEM), vmem] + [hbm] * 5,
        out_specs=(hbm, vmem),
        scratch_shapes=[
            pltpu.VMEM(w_up.shape, bf16),
            pltpu.VMEM(w_mid.shape, bf16),
            pltpu.VMEM(w_down.shape, bf16),
            pltpu.VMEM(sw_up.shape, bf16),
            pltpu.VMEM(sw_down.shape, bf16),
            pltpu.VMEM((3, lats // SUBLANES, levels * SUBLANES, LANES), jnp.float32),
            pltpu.VMEM((3, peers, levels, n_columns), bf16),
            pltpu.VMEM((3, peers, levels, n_columns), bf16),
            pltpu.VMEM((groups, rows, LANES), bf16),
            pltpu.VMEM((groups, rows, LANES), bf16),
            pltpu.VMEM((groups, rows, n_features), bf16),
            pltpu.VMEM((groups, rows, n_features), bf16),
            pltpu.VMEM((groups, rows, n_features), bf16),
            pltpu.VMEM((groups, rows, n_features), bf16),
            pltpu.VMEM((2, n_columns, levels * peers), jnp.float32),
            pltpu.SemaphoreType.DMA((5,)),
            pltpu.SemaphoreType.DMA((4,)),
            pltpu.SemaphoreType.DMA,
            pltpu.SemaphoreType.DMA((3,)),
            pltpu.SemaphoreType.DMA((3,)),
            pltpu.SemaphoreType.DMA((groups + 2,)),
        ],
        compiler_params=pltpu.CompilerParams(collective_id=0, has_side_effects=True),
    )(tracers, layer_mass, courant, remap, cost_class, spans.reshape(1, -1), b_up, w_up, w_mid, w_down, sw_up, sw_down)
    out = mixing + update.astype(jnp.float32)
    return out.reshape(2, lats, width, levels * peers).transpose(0, 3, 1, 2)


def shards(groups, peers, *args):
    levels, lats, lons = args[1].shape
    fits = (
        lons == LANES
        and peers == SUBLANES
        and levels % PACK == 0
        and lats % PACK == 0
        and lons // peers == BLK
        and levels * peers == LANES
    )
    return shards_kernel(groups, peers, *args) if fits else shards_plain(*args)


def solution(mesh):
    placed = (
        P(None, "lev", "lat", None),
        P("lev", "lat", None),
        P("lev", "lat"),
        P(),
        P("lat", "lev"),
        P(("lat", "lev"), None),
        P("lat", None, None),
        P("lat", None),
        P("lat", None, None),
        P("lat", None, None),
        P("lat", None, None),
        P("lat", None, None),
    )
    return jax.shard_map(
        functools.partial(shards, mesh.shape["lat"], mesh.shape["lev"]), mesh=mesh, in_specs=placed, out_specs=P(None, None, "lat", "lev"), check_vma=False
    )
```

```python
import functools

import jax
import jax.numpy as jnp
from jax import lax
from jax.experimental import pallas as pl
from jax.experimental.pallas import tpu as pltpu
from jax.sharding import PartitionSpec as P

LEV = 128
SUBSTEPS = 4
BLK = 16


def minmod(first, second):
    return 0.5 * (jnp.sign(first) + jnp.sign(second)) * jnp.minimum(jnp.abs(first), jnp.abs(second))


def advect(fields, speeds):
    for substep in range(SUBSTEPS):
        east_cell = jnp.roll(fields, -1, axis=-1)
        west_cell = jnp.roll(fields, 1, axis=-1)
        slopes = minmod(east_cell - fields, fields - west_cell)
        fluxes = speeds * (fields + 0.5 * (1.0 - speeds) * slopes)
        fields = fields - (fluxes - jnp.roll(fluxes, 1, axis=-1))
    return fields


def remap_levels(remap, fields):
    masses = jnp.einsum("kl,flyx->fkyx", remap, fields, precision=lax.Precision.HIGHEST)
    return masses[1:] / masses[0]


def physics(features, layer_up, bias_up, layer_mid, layer_down, short_up, short_down):
    hidden = jax.nn.silu(
        jnp.dot(features, layer_up, preferred_element_type=jnp.float32) + bias_up
    ).astype(jnp.bfloat16)
    deeper = jax.nn.silu(jnp.dot(hidden, layer_mid, preferred_element_type=jnp.float32)).astype(
        jnp.bfloat16
    )
    main_out = jnp.dot(deeper, layer_down, preferred_element_type=jnp.float32)
    shortwave = jax.nn.silu(jnp.dot(features, short_up, preferred_element_type=jnp.float32)).astype(
        jnp.bfloat16
    )
    side_out = jnp.dot(shortwave, short_down, preferred_element_type=jnp.float32)
    return (main_out, side_out)


def shards_plain(
    tracers,
    layer_mass,
    courant,
    remap,
    cost_class,
    spans,
    w_up,
    b_up,
    w_mid,
    w_down,
    sw_up,
    sw_down,
):
    fields = jnp.concatenate([layer_mass[None], tracers * layer_mass[None]], axis=0)
    fields = advect(fields, courant[None, :, :, None])
    regrouped = lax.all_to_all(fields, "lev", split_axis=3, concat_axis=1, tiled=True)
    mixing = remap_levels(remap, regrouped)
    width = mixing.shape[2] * mixing.shape[3]
    n_blocks = width // BLK
    groups = lax.axis_size("lat")
    most_blocks = max(2, (n_blocks + groups - 1) // groups)
    slots = groups * most_blocks
    features = mixing.reshape(2 * LEV, width).T.astype(jnp.bfloat16)
    column_blocks = features.reshape(n_blocks, BLK * 2 * LEV)
    factor = cost_class.astype(jnp.float32) * 0.5
    target = spans[:, 0]
    positions = jnp.arange(n_blocks, dtype=jnp.int32)
    earlier = positions[:, None] > positions[None, :]
    same_net = target[:, None] == target[None, :]
    slot_rank = jnp.sum((earlier & same_net).astype(jnp.int32), axis=1)
    slot_id = target * most_blocks + slot_rank
    placing = (jnp.arange(slots, dtype=jnp.int32)[:, None] == slot_id[None, :]).astype(jnp.float32)
    outgoing = jnp.dot(
        placing.astype(jnp.bfloat16), column_blocks, preferred_element_type=jnp.float32
    )
    outgoing = outgoing.astype(jnp.bfloat16).reshape(groups, most_blocks * BLK, 2 * LEV)
    sent_factor = (
        jnp.dot(placing, factor, precision=lax.Precision.HIGHEST)
        .astype(jnp.bfloat16)
        .reshape(groups, most_blocks * BLK)
    )
    incoming, incoming_factor = (
        lax.all_to_all(outgoing, "lat", split_axis=0, concat_axis=0, tiled=True),
        lax.all_to_all(sent_factor, "lat", split_axis=0, concat_axis=0, tiled=True),
    )
    main_out, side_out = physics(
        incoming.reshape(slots * BLK, 2 * LEV),
        w_up[0],
        b_up[0],
        w_mid[0],
        w_down[0],
        sw_up[0],
        sw_down[0],
    )
    owner_sum = (
        main_out + incoming_factor.reshape(slots * BLK).astype(jnp.float32)[:, None] * side_out
    ).astype(jnp.bfloat16)
    returned = lax.all_to_all(
        owner_sum.reshape(groups, most_blocks * BLK, 2 * LEV),
        "lat",
        split_axis=0,
        concat_axis=0,
        tiled=True,
    )
    tendency = jnp.dot(
        placing.T.astype(jnp.bfloat16),
        returned.reshape(slots, BLK * 2 * LEV),
        preferred_element_type=jnp.float32,
    )
    tendency = tendency.astype(jnp.bfloat16).reshape(width, 2 * LEV)
    update = tendency.astype(jnp.float32).T.reshape(mixing.shape)
    return mixing + update


MESH = pl.DeviceIdType.MESH
LANES = 128
SUBLANES = 8
PACK = 16


def as_columns(rows):
    count, width = rows.shape
    shape = (width, width)
    on_diagonal = lax.broadcasted_iota(jnp.int32, shape, 0) == lax.broadcasted_iota(
        jnp.int32, shape, 1
    )
    return [
        jnp.sum(
            jnp.where(on_diagonal, jnp.broadcast_to(rows[i : i + 1, :], shape), 0.0),
            axis=1,
            keepdims=True,
        )
        for i in range(count)
    ]


def transport(fields, speeds):
    weight = 0.5 * speeds * (1.0 - speeds)
    for substep in range(SUBSTEPS):
        ahead = pltpu.roll(fields, LANES - 1, 1) - fields
        behind = fields - pltpu.roll(fields, 1, 1)
        slopes = jnp.maximum(jnp.minimum(ahead, behind), 0.0) + jnp.minimum(
            jnp.maximum(ahead, behind), 0.0
        )
        fluxes = speeds * fields + weight * slopes
        fields = fields - (fluxes - pltpu.roll(fluxes, 1, 1))
    return fields


def swap_groups(block, width):
    rows = block.shape[0]
    group = lax.broadcasted_iota(jnp.int32, (1, 1, LANES), 2) // width
    block = pltpu.roll(block, 0, 1, stride=width, stride_axis=0)
    block = block.reshape(rows // SUBLANES, SUBLANES, LANES)
    for bit in (1, 2, 4):
        moved = pltpu.roll(block, SUBLANES - bit, 1)
        block = jnp.where((group // bit) % 2 == 1, moved, block)
    block = block.reshape(rows, LANES)
    return pltpu.roll(block, 0, 1, stride=width, stride_axis=0)


def silu(v):
    half = 0.5 * v
    return half + half * jnp.tanh(half)


def step_kernel(
    groups,
    peers,
    most,
    tracers,
    layer_mass,
    courant,
    remap,
    cost_class,
    spans,
    b_up,
    w_up,
    w_mid,
    w_down,
    sw_up,
    sw_down,
    mixing_out,
    update_out,
    v_up,
    v_mid,
    v_down,
    v_sup,
    v_sdown,
    turned,
    packed,
    gathered,
    factor_out,
    factor_in,
    columns_out,
    columns_in,
    result_out,
    result_in,
    mixed,
    weight_sems,
    own_sems,
    lev_send,
    lev_recv,
    lat_send,
    lat_recv,
):
    levels, lats, _ = layer_mass.shape
    me, home = lax.axis_index("lev"), lax.axis_index("lat")
    width = LANES // peers
    n_columns = lats * width
    n_blocks = n_columns // BLK
    rows = most * BLK

    barrier = pltpu.get_barrier_semaphore()
    for o in range(1, peers):
        pl.semaphore_signal(
            barrier, inc=1, device_id={"lev": lax.rem(me + o, peers)}, device_id_type=MESH
        )
    for o in range(1, groups):
        pl.semaphore_signal(
            barrier, inc=1, device_id={"lat": lax.rem(home + o, groups)}, device_id_type=MESH
        )
    weights = [
        pltpu.make_async_copy(source, held, weight_sems.at[i])
        for i, (source, held) in enumerate(
            ((w_up, v_up), (sw_up, v_sup), (w_mid, v_mid), (w_down, v_down), (sw_down, v_sdown))
        )
    ]
    for copy in weights:
        copy.start()

    speed = jnp.concatenate(
        [jnp.broadcast_to(column, (lats, LANES)) for column in as_columns(courant[...])], axis=0
    )
    mass = layer_mass[...].reshape(levels * lats, LANES)
    side = me // (peers // 2)
    others = []
    for k in range(peers - 1):
        low = peers - 1 - k
        low = low - (low <= me).astype(jnp.int32)
        high = k + (k >= me).astype(jnp.int32)
        others.append(side * high + (1 - side) * low)
    own_lev = []
    for f in range(3):
        field = mass
        if f:
            field = tracers[f - 1].reshape(levels * lats, LANES) * mass
        field = swap_groups(transport(field, speed), width)
        field = field.reshape(levels, lats // SUBLANES, SUBLANES, LANES)
        for half in range(lats // SUBLANES):
            turned[f, half] = field[:, half].reshape(levels * SUBLANES, LANES)
        for d in range(peers):
            for half in range(lats // SUBLANES):
                packed[f, d, :, half * LANES : (half + 1) * LANES] = turned[
                    f, half, pl.ds(d, levels, stride=SUBLANES), :
                ].astype(jnp.bfloat16)
        if f == 0:
            pl.semaphore_wait(barrier, peers - 1 + groups - 1)
        for to in others:
            copy = pltpu.make_async_remote_copy(
                src_ref=packed.at[f, lax.rem(peers - to, peers)],
                dst_ref=gathered.at[f, me],
                send_sem=lev_send,
                recv_sem=lev_recv.at[f],
                device_id={"lev": to},
                device_id_type=MESH,
            )
            copy.start()
        own = pltpu.make_async_copy(
            packed.at[f, lax.rem(peers - me, peers)], gathered.at[f, me], own_sems.at[f]
        )
        own.start()
        own_lev.append(own)
    named = [spans[0, b] for b in range(n_blocks)]
    slot = []
    for b in range(n_blocks):
        rank = jnp.int32(0)
        for earlier in range(b):
            rank = rank + (named[earlier] == named[b]).astype(jnp.int32)
        slot.append((named[b] * most + rank) * BLK)
    lane = lax.broadcasted_iota(jnp.int32, (1, n_columns), 1)
    row_of = jnp.zeros((1, n_columns), jnp.int32)
    for b in range(n_blocks):
        row_of = jnp.where(lane // BLK == b, slot[b], row_of)
    row_of = row_of + lane % BLK
    spread = (groups * rows, n_columns)
    placing = jnp.where(lax.broadcasted_iota(jnp.int32, spread, 0) == row_of, 1.0, 0.0).astype(
        jnp.bfloat16
    )
    offset = lax.broadcasted_iota(jnp.int32, (BLK, groups * rows), 1) - lax.broadcasted_iota(
        jnp.int32, (BLK, groups * rows), 0
    )
    restoring = jnp.concatenate(
        [jnp.where(offset == slot[b], 1.0, 0.0) for b in range(n_blocks)], axis=0
    ).astype(jnp.bfloat16)
    day = jnp.concatenate(
        [
            jnp.broadcast_to(column, (width, LANES))
            for column in as_columns(cost_class[...].astype(jnp.float32) * 0.5)
        ],
        axis=0,
    ).astype(jnp.bfloat16)
    factor_out[...] = (
        jnp.dot(placing, day, preferred_element_type=jnp.float32)
        .astype(jnp.bfloat16)
        .reshape(factor_out.shape)
    )

    turn = 1 - 2 * lax.rem(home, 2)
    partners = [lax.rem(home + turn * o + groups * groups, groups) for o in range(groups - 1, 0, -1)]

    def send(stage, source, landing, arrival, to):
        copy = pltpu.make_async_remote_copy(
            src_ref=source.at[to],
            dst_ref=landing.at[home],
            send_sem=lat_send.at[stage],
            recv_sem=arrival,
            device_id={"lat": to},
            device_id_type=MESH,
        )
        copy.start()

    def all_partners(stage, source, landing, arrival):
        return pltpu.make_async_remote_copy(
            src_ref=source.at[pl.ds(0, groups - 1)],
            dst_ref=landing.at[pl.ds(0, groups - 1)],
            send_sem=lat_send.at[stage],
            recv_sem=arrival,
            device_id={"lat": partners[0]},
            device_id_type=MESH,
        )

    for to in partners:
        send(0, factor_out, factor_in, lat_recv.at[groups], to)
    weight = remap[...].astype(jnp.bfloat16)
    target = []
    for f in range(3):
        own_lev[f].wait()
        pltpu.make_async_remote_copy(
            src_ref=packed.at[f, pl.ds(0, peers - 1)],
            dst_ref=gathered.at[f, pl.ds(0, peers - 1)],
            send_sem=lev_send,
            recv_sem=lev_recv.at[f],
            device_id={"lev": others[0]},
            device_id_type=MESH,
        ).wait_recv()
        target.append(
            lax.dot_general(
                gathered[f].reshape(peers * levels, n_columns),
                weight,
                (((0,), (1,)), ((), ())),
                preferred_element_type=jnp.float32,
            )
        )
    inverse = 1.0 / target[0]
    mixing = jnp.concatenate([target[1] * inverse, target[2] * inverse], axis=1)
    columns_out[...] = (
        jnp.dot(placing, mixing.astype(jnp.bfloat16), preferred_element_type=jnp.float32)
        .astype(jnp.bfloat16)
        .reshape(columns_out.shape)
    )
    for to in partners:
        send(1, columns_out, columns_in, lat_recv.at[home], to)
    for t in range(2):
        mixed[t] = mixing[:, t * LANES : (t + 1) * LANES]
    own_mixed = pltpu.make_async_copy(mixed, mixing_out, own_sems.at[3])
    own_mixed.start()
    for copy in weights:
        copy.wait()

    def dot(a, b):
        return jnp.dot(a, b[0], preferred_element_type=jnp.float32)

    def nets(features, scale):
        hidden = silu(dot(features, v_up) + b_up[...]).astype(jnp.bfloat16)
        shortwave = silu(dot(features, v_sup)).astype(jnp.bfloat16)
        deeper = silu(dot(hidden, v_mid)).astype(jnp.bfloat16)
        scale = jnp.concatenate([scale.astype(jnp.float32)] * (mixing.shape[1] // LANES), axis=1)
        return (dot(deeper, v_down) + scale * dot(shortwave, v_sdown)).astype(jnp.bfloat16)

    result_in[home] = nets(columns_out[home], factor_out[home])
    all_partners(0, factor_out, factor_in, lat_recv.at[groups]).wait_recv()
    for batch in (partners[:1], partners[1:]):
        for source in batch:
            pltpu.make_async_remote_copy(
                src_ref=columns_out.at[source],
                dst_ref=columns_in.at[source],
                send_sem=lat_send.at[1],
                recv_sem=lat_recv.at[source],
                device_id={"lat": source},
                device_id_type=MESH,
            ).wait_recv()
        result = nets(
            jnp.concatenate([columns_in[source] for source in batch], axis=0),
            jnp.concatenate([factor_in[source] for source in batch], axis=0),
        )
        for i, source in enumerate(batch):
            result_out[source] = result[i * rows : (i + 1) * rows]
            send(2, result_out, result_in, lat_recv.at[groups + 1], source)
    all_partners(2, result_out, result_in, lat_recv.at[groups + 1]).wait_recv()
    update = jnp.dot(
        restoring,
        result_in[...].reshape(groups * rows, mixing.shape[1]),
        preferred_element_type=jnp.float32,
    )
    for t in range(2):
        update_out[t] = update[:, t * LANES : (t + 1) * LANES].astype(jnp.bfloat16)
    own_mixed.wait()
    all_partners(0, factor_out, factor_in, lat_recv.at[groups]).wait_send()
    all_partners(1, columns_out, columns_in, lat_recv.at[groups]).wait_send()
    all_partners(2, result_out, result_in, lat_recv.at[groups]).wait_send()
    pltpu.make_async_remote_copy(
        src_ref=packed.at[:, pl.ds(0, peers - 1)],
        dst_ref=gathered.at[:, pl.ds(0, peers - 1)],
        send_sem=lev_send,
        recv_sem=lev_recv.at[0],
        device_id={"lev": others[0]},
        device_id_type=MESH,
    ).wait_send()


def shards_kernel(groups, peers, tracers, layer_mass, courant, remap, cost_class, spans, w_up, b_up, w_mid, w_down, sw_up, sw_down):
    levels, lats, lons = layer_mass.shape
    width = lons // peers
    n_columns = lats * width
    n_blocks = n_columns // BLK
    most = max(2, (n_blocks + groups - 1) // groups)
    rows = most * BLK
    n_features = 2 * levels * peers
    bf16 = jnp.bfloat16
    vmem = pl.BlockSpec(memory_space=pltpu.VMEM)
    hbm = pl.BlockSpec(memory_space=pl.ANY)
    mixing, update = pl.pallas_call(
        functools.partial(step_kernel, groups, peers, most),
        out_shape=(
            jax.ShapeDtypeStruct((2, n_columns, levels * peers), jnp.float32),
            jax.ShapeDtypeStruct((2, n_columns, levels * peers), bf16),
        ),
        in_specs=[vmem] * 5 + [pl.BlockSpec(memory_space=pltpu.SMEM), vmem] + [hbm] * 5,
        out_specs=(hbm, vmem),
        scratch_shapes=[
            pltpu.VMEM(w_up.shape, bf16),
            pltpu.VMEM(w_mid.shape, bf16),
            pltpu.VMEM(w_down.shape, bf16),
            pltpu.VMEM(sw_up.shape, bf16),
            pltpu.VMEM(sw_down.shape, bf16),
            pltpu.VMEM((3, lats // SUBLANES, levels * SUBLANES, LANES), jnp.float32),
            pltpu.VMEM((3, peers, levels, n_columns), bf16),
            pltpu.VMEM((3, peers, levels, n_columns), bf16),
            pltpu.VMEM((groups, rows, LANES), bf16),
            pltpu.VMEM((groups, rows, LANES), bf16),
            pltpu.VMEM((groups, rows, n_features), bf16),
            pltpu.VMEM((groups, rows, n_features), bf16),
            pltpu.VMEM((groups, rows, n_features), bf16),
            pltpu.VMEM((groups, rows, n_features), bf16),
            pltpu.VMEM((2, n_columns, levels * peers), jnp.float32),
            pltpu.SemaphoreType.DMA((5,)),
            pltpu.SemaphoreType.DMA((4,)),
            pltpu.SemaphoreType.DMA,
            pltpu.SemaphoreType.DMA((3,)),
            pltpu.SemaphoreType.DMA((3,)),
            pltpu.SemaphoreType.DMA((groups + 2,)),
        ],
        compiler_params=pltpu.CompilerParams(collective_id=0, has_side_effects=True, vmem_limit_bytes=16 * 1024 * 1024),
    )(
        *(
            pltpu.with_memory_space_constraint(array, pltpu.HBM)
            for array in (
                tracers,
                layer_mass,
                courant,
                remap,
                cost_class,
                spans.reshape(1, -1),
                b_up,
                w_up,
                w_mid,
                w_down,
                sw_up,
                sw_down,
            )
        )
    )
    out = mixing + update.astype(jnp.float32)
    return out.reshape(2, lats, width, levels * peers).transpose(0, 3, 1, 2)


def shards(groups, peers, *args):
    levels, lats, lons = args[1].shape
    fits = (
        lons == LANES
        and peers == SUBLANES
        and levels % PACK == 0
        and lats % PACK == 0
        and lons // peers == BLK
        and levels * peers == LANES
    )
    return shards_kernel(groups, peers, *args) if fits else shards_plain(*args)


def solution(mesh):
    placed = (
        P(None, "lev", "lat", None),
        P("lev", "lat", None),
        P("lev", "lat"),
        P(),
        P("lat", "lev"),
        P(("lat", "lev"), None),
        P("lat", None, None),
        P("lat", None),
        P("lat", None, None),
        P("lat", None, None),
        P("lat", None, None),
        P("lat", None, None),
    )
    return jax.shard_map(
        functools.partial(shards, mesh.shape["lat"], mesh.shape["lev"]), mesh=mesh, in_specs=placed, out_specs=P(None, None, "lat", "lev"), check_vma=False
    )
```
